32 devices in a mesh: groups: 2 (over x), pb: 8 (over z, y), ka: 2 (over core).
Axes of the slice: x: 2, y: 2, z: 4, core: 2. Of those that a mesh axis runs over, the one named last changes fastest.
Arguments:
- queries: bfloat16 [12288, 256], P(('groups', 'pb', 'ka')), parts along dimension 0, may hold values from -6 to 6
- keys: bfloat16 [12288, 256], P(('groups', 'pb', 'ka')), parts along dimension 0, may hold values from -6 to 6
- values: bfloat16 [12288, 256], P(('groups', 'pb', 'ka')), parts along dimension 0, may hold values from -96 to 96
- block_pairs: int32 [4, 8, 16, 9], P('groups', 'pb'), parts along dimension 0, may hold values from -1 to 17, as said below
Outputs:
- attended: bfloat16 [12288, 256], P(('groups', 'pb', 'ka')), parts along dimension 0
The draws below stay inside these ranges and needn't reach their ends.
There are 2 independent parts, one for each index of `groups`. The reference program is written for one: setup_inputs(seed, part) draws one part's arguments, and reference() takes and returns one part's arrays. A program takes and returns all parts, laid end to end along the dimension named above; each array names one. Nothing has to cross between parts.
Inputs may be any that keep to these rules, and one draw needn't show every extreme that they name: Each list block_pairs[h, p, s, :] holds 1 to 9 distinct codes (as defined in the reference program) followed by entries -1; in every draw some list holds 9 codes. Every query block's pair with the key block of the same tokens is kept for every head.
All inputs are finite; a program needn't handle non-finite values.
Results may differ from the reference program's by a relative error of at most 0.0085.
Values may be sent and summed in bfloat16 or wider, within the bound.
A program may use at most 128 MiB of HBM per device.

```python
import jax
import jax.numpy as jnp
from jax import lax

HEAD = 128
HEADS = 2
BLOCK = 128
TOK_DEV = 384
MOST = 9
TOKENS = 6144
N_PB = 8
N_KA = 2


def base_field(key):
    field_shape = (TOKENS, HEADS * HEAD)
    matrix = jax.random.normal(jax.random.fold_in(key, 2), field_shape, jnp.float32)
    return jnp.clip(matrix, -6.0, 6.0)


def draw_queries(key, part):
    matrix = base_field(jax.random.fold_in(key, 11))
    return matrix.astype(jnp.bfloat16)


def draw_keys(key, part):
    matrix = base_field(jax.random.fold_in(key, 12))
    return matrix.astype(jnp.bfloat16)


def draw_block_pairs(key, part):
    shard_count = N_PB * N_KA
    shard_blocks = TOK_DEV // BLOCK
    grid_size = N_KA * shard_blocks * shard_blocks
    levels = jax.random.randint(jax.random.fold_in(key, 21), (HEADS, N_PB, 1, N_KA), 0, 3)
    levels = jnp.broadcast_to(levels, (HEADS, N_PB, N_PB, N_KA)).reshape(HEADS, N_PB, shard_count)
    counts = jax.random.randint(jax.random.fold_in(key, 22), (HEADS, N_PB, shard_count), 1, MOST // 2 + 1)
    counts = counts + levels * (MOST // 4)
    tile_ids = jnp.arange(N_PB)[:, None]
    shard_ids = jnp.arange(shard_count)[None, :]
    own_shard = shard_ids // N_KA == tile_ids
    counts = jnp.where(own_shard[None], jnp.maximum(counts, shard_blocks + 1), counts)
    flat_ids = jnp.arange(N_PB * shard_count).reshape(N_PB, shard_count)
    chosen = jax.random.randint(jax.random.fold_in(key, 23), (HEADS, 1, 1), 0, N_PB * shard_count)
    counts = jnp.minimum(jnp.where(flat_ids[None] == chosen, MOST, counts), MOST)
    places = jnp.arange(grid_size)
    query_local = places // shard_blocks
    key_local = places % shard_blocks
    diagonal = (shard_ids[:, :, None] == tile_ids[:, :, None] * N_KA + (query_local // shard_blocks)[None, None, :]) & (key_local == query_local % shard_blocks)[None, None, :]
    jitter = jax.random.randint(jax.random.fold_in(key, 24), (HEADS, N_PB, shard_count, grid_size), 0, 1 << 16)
    priority = jitter * 1024 + places + diagonal[None].astype(jnp.int32) * (1 << 28)
    ranked = jnp.argsort(-priority, axis=-1, stable=True)[..., :MOST]
    slot_ids = jnp.arange(MOST)
    return jnp.where(slot_ids < counts[..., None], ranked, -1).astype(jnp.int32)


def block_scale(key, extent, split, low, high):
    gain, own = 1.0, jax.random.fold_in(key, 6)
    for dim, blocks in split:
        draws = jnp.exp(jax.random.uniform(jax.random.fold_in(own, dim), (blocks,), jnp.float32, low / len(split), high / len(split)))
        gain = gain * jnp.repeat(draws, extent[dim] // blocks).reshape([-1 if axis == dim else 1 for axis in range(len(extent))])
    return gain


def scatter_about(stream_key, dims, width, reach, cuts=(), kind=jnp.bfloat16):
    result = width * jax.random.normal(stream_key, dims, jnp.float32)
    if cuts:
        result = result * block_scale(stream_key, dims, cuts, -0.22, 0.18)
    return jnp.clip(result, -reach, reach).astype(kind)


def setup_inputs(seed: int = 0, part: int = 0) -> dict:
    splits = jax.random.split(jax.random.key(seed), 5)
    part_splits = jax.random.split(jax.random.fold_in(splits[4], part), 5)
    return {
        "queries": draw_queries(jax.random.fold_in(jax.random.fold_in(splits[4], part), 71), part),
        "keys": draw_keys(jax.random.fold_in(jax.random.fold_in(splits[4], part), 71), part),
        "values": scatter_about(part_splits[2], (TOKENS, HEADS * HEAD), 16.0, 96.0, ((0, 16),)),
        "block_pairs": draw_block_pairs(jax.random.fold_in(jax.random.fold_in(splits[4], part), 71), part),
    }


NEGATIVE_FILL = -1.0e30


def tile_attention(queries, keys, values, block_pairs, head_index, tile_index):
    shard_blocks = TOK_DEV // BLOCK
    tile_rows = N_KA * TOK_DEV
    tile_blocks = N_KA * shard_blocks
    shard_count = N_PB * N_KA
    per_head = lax.dynamic_index_in_dim(block_pairs, head_index, 0, keepdims=False)
    pair_codes = lax.dynamic_index_in_dim(per_head, tile_index, 0, keepdims=False).reshape(-1)
    active = pair_codes >= 0
    clean = jnp.where(active, pair_codes, 0).astype(jnp.int32)
    query_block = (clean // shard_blocks).astype(jnp.int32)
    shard_of = jnp.arange(shard_count * MOST, dtype=jnp.int32) // MOST
    key_block = (shard_of * shard_blocks + clean % shard_blocks).astype(jnp.int32)
    column_start = (head_index * HEAD).astype(jnp.int32)
    row_start = (tile_index * tile_rows).astype(jnp.int32)
    query_tile = lax.dynamic_slice(queries, (row_start, column_start), (tile_rows, HEAD))
    key_cols = lax.dynamic_slice_in_dim(keys, column_start, HEAD, 1).reshape(TOKENS // BLOCK, BLOCK, HEAD)
    value_cols = lax.dynamic_slice_in_dim(values, column_start, HEAD, 1).reshape(TOKENS // BLOCK, BLOCK, HEAD)
    query_sel = query_tile.reshape(tile_blocks, BLOCK, HEAD)[query_block].astype(jnp.float32)
    key_sel = key_cols[key_block].astype(jnp.float32)
    value_sel = value_cols[key_block].astype(jnp.float32)
    scores = jnp.einsum("nqd,nkd->nqk", query_sel, key_sel, precision=lax.Precision.HIGHEST) * (HEAD ** -0.5)
    scores = jnp.where(active[:, None, None], scores, NEGATIVE_FILL)
    slot_max = scores.max(-1)
    is_kept_pair = (query_block[:, None] == jnp.arange(tile_blocks, dtype=jnp.int32)[None, :]) & active[:, None]
    peak = jnp.where(is_kept_pair[:, :, None], slot_max[:, None, :], NEGATIVE_FILL).max(0)
    slot_peak = peak[query_block]
    chances = jnp.where(active[:, None, None], jnp.exp(scores - slot_peak[:, :, None]), 0.0)
    pair_flag = is_kept_pair.astype(jnp.float32)
    total = jnp.einsum("nb,nq->bq", pair_flag, chances.sum(-1), precision=lax.Precision.HIGHEST)
    softmax_weight = lax.optimization_barrier(chances.astype(jnp.bfloat16)).astype(jnp.float32)
    partial_output = jnp.einsum("nqk,nkd->nqd", softmax_weight, value_sel, precision=lax.Precision.HIGHEST)
    running_output = jnp.einsum("vw,vhs->whs", pair_flag, partial_output, precision=lax.Precision.HIGHEST)
    return (running_output / total[:, :, None]).astype(jnp.bfloat16).reshape(tile_rows, HEAD)


def reference(queries, keys, values, block_pairs):
    head_numbers = jnp.repeat(jnp.arange(HEADS, dtype=jnp.int32), N_PB)
    tile_ids = jnp.tile(jnp.arange(N_PB, dtype=jnp.int32), HEADS)

    def one_tile(index_pair):
        return tile_attention(queries, keys, values, block_pairs, index_pair[0], index_pair[1])

    tile_outputs = lax.map(one_tile, (head_numbers, tile_ids))
    tile_outputs = tile_outputs.reshape(HEADS, N_PB, N_KA * TOK_DEV, HEAD).transpose(1, 2, 0, 3)
    return tile_outputs.reshape(TOKENS, HEADS * HEAD)
```

```python
import functools
import math

import jax
import jax.numpy as jnp
from jax import lax
from jax.experimental import pallas as pl
from jax.experimental.pallas import tpu as pltpu
from jax.sharding import PartitionSpec as P

HEAD = 128
HEADS = 2
BLOCK = 128
NEGATIVE_FILL = -1e30
EXP2_SCALE = HEAD ** (-0.5) * math.log2(math.e)
MESH = pl.DeviceIdType.MESH
LEFT, RIGHT, ACROSS = 0, 1, 2


def kernel(
    n_pb, n_ka, width, q_ref, k_ref, v_ref, pairs_ref, out_ref,
    qbuf, kbuf, vbuf, bias, peak, total, accum, obuf,
    send_sem, recv_sem, local_sem, swap_send, swap_recv,
):
    rows = q_ref.shape[0]
    tile = n_ka * rows
    cut = rows - BLOCK
    n_y = width
    n_z = n_pb // n_y
    core = lax.axis_index("ka")
    place = lax.axis_index("pb")
    z, y = place // n_y, place % n_y
    other = 1 - core
    across = z * n_y + (1 - y)
    has_left, has_right = z > 0, z < n_z - 1
    targets = {LEFT: place - n_y, RIGHT: place + n_y, ACROSS: across}

    barrier = pltpu.get_barrier_semaphore()
    pl.semaphore_signal(barrier, inc=1, device_id={"ka": other}, device_id_type=MESH)
    pl.semaphore_signal(barrier, inc=1, device_id={"pb": across}, device_id_type=MESH)

    @pl.when(has_left)
    def _():
        pl.semaphore_signal(barrier, inc=1, device_id={"pb": place - n_y}, device_id_type=MESH)

    @pl.when(has_right)
    def _():
        pl.semaphore_signal(barrier, inc=1, device_id={"pb": place + n_y}, device_id_type=MESH)

    my_columns = pl.ds(pl.multiple_of(core * HEAD, HEAD), HEAD)
    other_columns = pl.ds(pl.multiple_of(other * HEAD, HEAD), HEAD)
    my_rows = pl.ds(pl.multiple_of(core * rows, BLOCK), rows)
    other_rows = pl.ds(pl.multiple_of(other * rows, BLOCK), rows)

    stage = [
        pltpu.make_async_copy(k_ref.at[:, my_columns], kbuf.at[place, my_rows], local_sem.at[0]),
        pltpu.make_async_copy(v_ref.at[:, my_columns], vbuf.at[place, my_rows], local_sem.at[1]),
        pltpu.make_async_copy(q_ref.at[:, my_columns], qbuf.at[my_rows], local_sem.at[2]),
    ]
    for item in stage:
        item.start()

    codes = pairs_ref[core, 0]
    shards = codes.shape[0]
    query_block = lax.broadcasted_iota(jnp.int32, (shards, tile), 1) // BLOCK
    blocks = rows // BLOCK
    kept = [None] * blocks
    for slot in range(codes.shape[1]):
        column = jnp.broadcast_to(codes[:, slot : slot + 1], (shards, tile))
        for j in range(blocks):
            hit = column == query_block * blocks + j
            kept[j] = hit if kept[j] is None else kept[j] | hit
    for j in range(blocks):
        bias[j] = jnp.where(kept[j], 0.0, NEGATIVE_FILL).astype(jnp.float32)
    peak[...] = jnp.full_like(peak, NEGATIVE_FILL)
    total[...] = jnp.zeros_like(total)
    accum[...] = jnp.zeros_like(accum)

    pl.semaphore_wait(
        barrier, 2 + has_left.astype(jnp.int32) + has_right.astype(jnp.int32)
    )

    def swap(index, source, target):
        return pltpu.make_async_remote_copy(
            src_ref=source, dst_ref=target, send_sem=swap_send.at[index],
            recv_sem=swap_recv.at[index], device_id={"ka": other}, device_id_type=MESH,
        )

    swaps_out = [
        swap(0, k_ref.at[:, other_columns], kbuf.at[place, my_rows]),
        swap(1, v_ref.at[:, other_columns], vbuf.at[place, my_rows]),
        swap(2, q_ref.at[:, other_columns], qbuf.at[my_rows]),
    ]
    for item in swaps_out:
        item.start()

    def part(p, a, m):
        base = pl.multiple_of(a * rows, BLOCK)
        if m == 0:
            return kbuf.at[p, pl.ds(base, rows)]
        if m == 1:
            return vbuf.at[p, pl.ds(base, cut)]
        return vbuf.at[p, pl.ds(pl.multiple_of(base + cut, BLOCK), BLOCK)]

    def message(way, p, a, m):
        ref = part(p, a, m)
        return pltpu.make_async_remote_copy(
            src_ref=ref, dst_ref=ref, send_sem=send_sem.at[way, p, a, m],
            recv_sem=recv_sem.at[p, a, m], device_id={"pb": targets[way]}, device_id_type=MESH,
        )

    def send(way, p, a, m):
        if way == ACROSS:
            message(way, p, a, m).start()
        else:
            @pl.when(has_left if way == LEFT else has_right)
            def _():
                message(way, p, a, m).start()

    def arrive(p, a, m):
        message(ACROSS, p, a, m).wait_recv()

    def send_own(a, parts):
        for m in parts:
            for way in (ACROSS, LEFT, RIGHT):
                send(way, place, a, m)

    stage[0].wait()
    send_own(core, (0,))
    stage[1].wait()
    send_own(core, (2, 1))
    swap(0, k_ref.at[:, other_columns], kbuf.at[place, other_rows]).wait_recv()
    send_own(other, (0,))
    swap(1, v_ref.at[:, other_columns], vbuf.at[place, other_rows]).wait_recv()
    send_own(other, (2, 1))
    stage[2].wait()
    swap(2, q_ref.at[:, other_columns], qbuf.at[other_rows]).wait_recv()

    lanes = 256 if tile % 256 == 0 else 128

    def attend(p):
        for start in range(0, tile, lanes):
            span = pl.ds(start, lanes)
            scores = lax.dot_general(
                kbuf[p], qbuf[span, :], (((1,), (1,)), ((), ())),
                preferred_element_type=jnp.float32,
            )
            masked = []
            for a in range(n_ka):
                for j in range(blocks):
                    row = (a * blocks + j) * BLOCK
                    line = bias[j, pl.ds(p * n_ka + a, 1), span]
                    masked.append(scores[row : row + BLOCK] + line)
            scores = jnp.concatenate(masked, axis=0)
            before = peak[:, span]
            after = jnp.maximum(before, scores.max(0, keepdims=True))
            rescale = jnp.exp2((before - after) * EXP2_SCALE)
            chances = jnp.exp2((scores - after) * EXP2_SCALE)
            peak[:, span] = after
            total[:, span] = total[:, span] * rescale + chances.sum(0, keepdims=True)
            accum[:, span] = accum[:, span] * rescale + lax.dot_general(
                vbuf[p], chances.astype(jnp.bfloat16), (((0,), (0,)), ((), ())),
                preferred_element_type=jnp.float32,
            )

    attend(place)

    for a in range(n_ka):
        arrive(across, a, 2)
        send(LEFT, across, a, 2)
        send(RIGHT, across, a, 2)

    def sides(step):
        return ((z - step, z - step >= 0, RIGHT), (z + step, z + step < n_z, LEFT))

    def attend_across(p):
        for a in range(n_ka):
            arrive(p, a, 0)
            arrive(p, a, 1)
        attend(p)

    def forward(step):
        for a in range(n_ka):
            for m in (0, 1):
                for far, valid, way in sides(step):
                    @pl.when(valid)
                    def _(far=far, way=way):
                        p = far * n_y + y
                        arrive(p, a, m)
                        send(way, p, a, m)
                        send(ACROSS, p, a, m)
            for far, valid, way in sides(step):
                @pl.when(valid)
                def _(far=far, way=way):
                    for near in (y, 1 - y):
                        p = far * n_y + near
                        arrive(p, a, 2)
                        send(way, p, a, 2)

    forward(1)
    attend_across(across)

    def one_step(step, carry):
        for far, valid, _ in sides(step):
            @pl.when(valid)
            def _(far=far):
                attend(far * n_y + y)

        @pl.when(step < n_z - 1)
        def _():
            forward(step + 1)

        for far, valid, _ in sides(step):
            @pl.when(valid)
            def _(far=far):
                attend_across(far * n_y + 1 - y)
        return carry

    lax.fori_loop(1, n_z, one_step, 0)

    def finish(which):
        span = pl.ds(pl.multiple_of(which * rows, BLOCK), rows)
        done = accum[:, span] / total[:, span]
        obuf[span, :] = done.T.astype(obuf.dtype)

    finish(other)
    give = pltpu.make_async_remote_copy(
        src_ref=obuf.at[other_rows], dst_ref=out_ref.at[:, my_columns],
        send_sem=swap_send.at[3], recv_sem=swap_recv.at[3],
        device_id={"ka": other}, device_id_type=MESH,
    )
    give.start()
    finish(core)
    keep = pltpu.make_async_copy(obuf.at[my_rows], out_ref.at[:, my_columns], local_sem.at[3])
    keep.start()

    def drain(way, far, near, a, m):
        message(way, far * n_y + near, a, m).wait_send()

    def drain_line(way):
        def body(far, carry):
            for a in range(n_ka):
                for m in (0, 1):
                    drain(way, far, y, a, m)
                for near in range(n_y):
                    drain(way, far, near, a, 2)
            return carry
        return body

    lax.fori_loop(jnp.where(has_left, z, n_z), n_z, drain_line(LEFT), 0)
    lax.fori_loop(0, jnp.where(has_right, z + 1, 0), drain_line(RIGHT), 0)

    def drain_across(far, carry):
        for a in range(n_ka):
            for m in (0, 1):
                drain(ACROSS, far, y, a, m)
        return carry

    lax.fori_loop(0, n_z, drain_across, 0)
    for a in range(n_ka):
        drain(ACROSS, z, y, a, 2)
    for item in swaps_out:
        item.wait_send()
    give.wait_send()
    keep.wait()
    pltpu.make_async_remote_copy(
        src_ref=obuf.at[other_rows], dst_ref=out_ref.at[:, other_columns],
        send_sem=swap_send.at[3], recv_sem=swap_recv.at[3],
        device_id={"ka": other}, device_id_type=MESH,
    ).wait_recv()


def solution(mesh):
    n_pb, n_ka = mesh.shape["pb"], mesh.shape["ka"]
    width = 2

    def local(queries, keys, values, block_pairs):
        rows = queries.shape[0]
        tile = n_ka * rows
        shards = block_pairs.shape[2]
        anywhere = pl.BlockSpec(memory_space=pl.ANY)
        return pl.pallas_call(
            functools.partial(kernel, n_pb, n_ka, width),
            out_shape=jax.ShapeDtypeStruct(queries.shape, queries.dtype),
            in_specs=[anywhere, anywhere, anywhere, pl.BlockSpec(memory_space=pltpu.VMEM)],
            out_specs=anywhere,
            scratch_shapes=[
                pltpu.VMEM((tile, HEAD), jnp.bfloat16),
                pltpu.VMEM((n_pb, tile, HEAD), jnp.bfloat16),
                pltpu.VMEM((n_pb, tile, HEAD), jnp.bfloat16),
                pltpu.VMEM((rows // BLOCK, shards, tile), jnp.float32),
                pltpu.VMEM((1, tile), jnp.float32),
                pltpu.VMEM((1, tile), jnp.float32),
                pltpu.VMEM((HEAD, tile), jnp.float32),
                pltpu.VMEM((tile, HEAD), jnp.bfloat16),
                pltpu.SemaphoreType.DMA((3, n_pb, n_ka, 3)),
                pltpu.SemaphoreType.DMA((n_pb, n_ka, 3)),
                pltpu.SemaphoreType.DMA((4,)),
                pltpu.SemaphoreType.DMA((4,)),
                pltpu.SemaphoreType.DMA((4,)),
            ],
            compiler_params=pltpu.CompilerParams(collective_id=0, has_side_effects=True),
        )(queries, keys, values, block_pairs)

    rows_spec = P(("groups", "pb", "ka"), None)
    return jax.shard_map(
        local, mesh=mesh,
        in_specs=(rows_spec, rows_spec, rows_spec, P("groups", "pb", None, None)),
        out_specs=rows_spec, check_vma=False,
    )
```

```python
import functools
import math

import jax
import jax.numpy as jnp
from jax import lax
from jax.experimental import pallas as pl
from jax.experimental.pallas import tpu as pltpu
from jax.sharding import PartitionSpec as P

HEAD = 128
HEADS = 2
BLOCK = 128
NEGATIVE_FILL = -1e30
EXP2_SCALE = HEAD ** (-0.5) * math.log2(math.e)
MESH = pl.DeviceIdType.MESH
LEFT, RIGHT, ACROSS = 0, 1, 2


def kernel(
    n_pb, n_ka, width, q_ref, k_ref, v_ref, pairs_ref, out_ref,
    qbuf, kbuf, vbuf, bias, peak, total, accum, obuf, qturned,
    send_sem, recv_sem, local_sem, swap_send, swap_recv,
):
    rows = q_ref.shape[0]
    tile = n_ka * rows
    late = BLOCK - BLOCK // 4
    half = (rows - late) // 2
    n_y = width
    n_z = n_pb // n_y
    core = lax.axis_index("ka")
    place = lax.axis_index("pb")
    z, y = place // n_y, place % n_y
    other = 1 - core
    across = z * n_y + (1 - y)
    has_left, has_right = z > 0, z < n_z - 1
    targets = {LEFT: place - n_y, RIGHT: place + n_y, ACROSS: across}

    barrier = pltpu.get_barrier_semaphore()
    pl.semaphore_signal(barrier, inc=1, device_id={"ka": other}, device_id_type=MESH)
    pl.semaphore_signal(barrier, inc=1, device_id={"pb": across}, device_id_type=MESH)

    @pl.when(has_left)
    def _():
        pl.semaphore_signal(barrier, inc=1, device_id={"pb": place - n_y}, device_id_type=MESH)

    @pl.when(has_right)
    def _():
        pl.semaphore_signal(barrier, inc=1, device_id={"pb": place + n_y}, device_id_type=MESH)

    my_columns = pl.ds(pl.multiple_of(core * HEAD, HEAD), HEAD)
    other_columns = pl.ds(pl.multiple_of(other * HEAD, HEAD), HEAD)
    my_rows = pl.ds(pl.multiple_of(core * rows, BLOCK), rows)
    other_rows = pl.ds(pl.multiple_of(other * rows, BLOCK), rows)

    stage = [
        pltpu.make_async_copy(k_ref.at[:, my_columns], kbuf.at[place, my_rows], local_sem.at[0]),
        pltpu.make_async_copy(v_ref.at[:, my_columns], vbuf.at[place, my_rows], local_sem.at[1]),
        pltpu.make_async_copy(q_ref.at[:, my_columns], qbuf.at[my_rows], local_sem.at[2]),
    ]
    for item in stage:
        item.start()

    pl.semaphore_wait(
        barrier, 2 + has_left.astype(jnp.int32) + has_right.astype(jnp.int32)
    )

    def swap(index, source, target):
        return pltpu.make_async_remote_copy(
            src_ref=source, dst_ref=target, send_sem=swap_send.at[index],
            recv_sem=swap_recv.at[index], device_id={"ka": other}, device_id_type=MESH,
        )

    swaps_out = [
        swap(0, k_ref.at[:, other_columns], kbuf.at[place, my_rows]),
        swap(1, v_ref.at[:, other_columns], vbuf.at[place, my_rows]),
        swap(2, q_ref.at[:, other_columns], qbuf.at[my_rows]),
    ]
    for item in swaps_out:
        item.start()

    spans = ((0, rows), (0, half), (half, half), (2 * half, late))
    early, last = (0, 1, 2), 3

    def part(p, a, m):
        start, size = spans[m]
        span = pl.ds(pl.multiple_of(a * rows + start, 16), size)
        return (vbuf if m else kbuf).at[p, span]

    def message(way, p, a, m, source=None):
        ref = part(p, a, m)
        return pltpu.make_async_remote_copy(
            src_ref=ref if source is None else source, dst_ref=ref, send_sem=send_sem.at[way, p, a, m],
            recv_sem=recv_sem.at[p, a, m], device_id={"pb": targets[way]}, device_id_type=MESH,
        )

    def send(way, p, a, m, source=None):
        if way == ACROSS:
            message(way, p, a, m, source).start()
        else:
            @pl.when(has_left if way == LEFT else has_right)
            def _():
                message(way, p, a, m, source).start()

    def arrive(p, a, m):
        message(ACROSS, p, a, m).wait_recv()

    def send_own(a, parts, source=None, ways=(ACROSS, LEFT, RIGHT)):
        for m in parts:
            start, size = spans[m]
            view = None if source is None else source.at[pl.ds(start, size), my_columns]
            for way in ways:
                send(way, place, a, m, view)

    send_own(core, (0,), k_ref)
    send_own(core, (last,), v_ref, (ACROSS,))
    send_own(core, (1, 2), v_ref)

    codes = pairs_ref[core, :, 0, :].T
    shards = codes.shape[0]
    query_block = lax.broadcasted_iota(jnp.int32, (shards, tile), 1) // BLOCK
    blocks = rows // BLOCK
    kept = [None] * blocks
    for slot in range(codes.shape[1]):
        column = jnp.broadcast_to(codes[:, slot : slot + 1], (shards, tile))
        for j in range(blocks):
            hit = column == query_block * blocks + j
            kept[j] = hit if kept[j] is None else kept[j] | hit
    for j in range(blocks):
        bias[j] = jnp.where(kept[j], 0.0, NEGATIVE_FILL).astype(jnp.float32)
    peak[...] = jnp.full_like(peak, NEGATIVE_FILL)
    total[...] = jnp.zeros_like(total)
    accum[...] = jnp.zeros_like(accum)

    swap(0, k_ref.at[:, other_columns], kbuf.at[place, other_rows]).wait_recv()
    send_own(other, (0,))
    swap(1, v_ref.at[:, other_columns], vbuf.at[place, other_rows]).wait_recv()
    send_own(other, (last,), None, (ACROSS,))
    send_own(other, (1, 2))
    send_own(core, (last,), v_ref, (LEFT, RIGHT))
    send_own(other, (last,), None, (LEFT, RIGHT))
    for item in stage:
        item.wait()
    swap(2, q_ref.at[:, other_columns], qbuf.at[other_rows]).wait_recv()

    qturned[...] = qbuf[...].T
    lanes = tile

    def attend(p, first=0, count=n_ka):
        keys = pl.ds(first * rows, count * rows)
        turned = vbuf[p, keys].T
        for start in range(0, tile, lanes):
            span = pl.ds(start, lanes)
            scores = lax.dot_general(
                kbuf[p, keys], qturned[:, span], (((1,), (0,)), ((), ())),
                preferred_element_type=jnp.float32,
            )
            masked = []
            for a in range(count):
                for j in range(blocks):
                    row = (a * blocks + j) * BLOCK
                    line = bias[j, pl.ds(p * n_ka + first + a, 1), span]
                    masked.append(scores[row : row + BLOCK] + line)
            scores = jnp.concatenate(masked, axis=0)
            before = peak[:, span]
            after = jnp.maximum(before, scores.max(0, keepdims=True))
            rescale = jnp.exp2((before - after) * EXP2_SCALE)
            chances = jnp.exp2((scores - after) * EXP2_SCALE)
            peak[:, span] = after
            total[:, span] = total[:, span] * rescale + chances.sum(0, keepdims=True)
            accum[:, span] = accum[:, span] * rescale + lax.dot_general(
                turned, chances.astype(jnp.bfloat16), (((1,), (0,)), ((), ())),
                preferred_element_type=jnp.float32,
            )

    attend(place)

    for a in range(n_ka):
        arrive(across, a, last)
        send(LEFT, across, a, last)
        send(RIGHT, across, a, last)

    def sides(step):
        return ((z - step, z - step >= 0, RIGHT), (z + step, z + step < n_z, LEFT))

    def attend_across(p):
        for a in range(n_ka):
            for m in early:
                arrive(p, a, m)
        attend(p)

    def forward_early(step):
        for a in range(n_ka):
            for m in early:
                for far, valid, way in sides(step):
                    @pl.when(valid)
                    def _(far=far, way=way):
                        p = far * n_y + y
                        arrive(p, a, m)
                        send(way, p, a, m)
                        send(ACROSS, p, a, m)

    def forward_last(step):
        for a in range(n_ka):
            for far, valid, way in sides(step):
                @pl.when(valid)
                def _(far=far, way=way):
                    for near in (y, 1 - y):
                        p = far * n_y + near
                        arrive(p, a, last)
                        send(way, p, a, last)

    def across_sides(step):
        for far, valid, _ in sides(step):
            @pl.when(valid)
            def _(far=far):
                attend_across(far * n_y + 1 - y)

    at_end = jnp.logical_not(jnp.logical_and(has_left, has_right))
    forward_early(1)
    forward_last(1)
    attend_across(across)

    def one_step(step, carry):
        for far, valid, _ in sides(step):
            @pl.when(valid)
            def _(far=far):
                attend(far * n_y + y)

        @pl.when(step < n_z - 1)
        def _():
            forward_early(step + 1)

        @pl.when(at_end)
        def _():
            across_sides(step)

        @pl.when(step < n_z - 1)
        def _():
            forward_last(step + 1)

        @pl.when(jnp.logical_not(at_end))
        def _():
            across_sides(step)
        return carry

    lax.fori_loop(1, n_z, one_step, 0)

    def finish(which):
        span = pl.ds(pl.multiple_of(which * rows, BLOCK), rows)
        done = accum[:, span] / total[:, span]
        obuf[span, :] = done.T.astype(obuf.dtype)

    finish(other)
    give = pltpu.make_async_remote_copy(
        src_ref=obuf.at[other_rows], dst_ref=out_ref.at[:, my_columns],
        send_sem=swap_send.at[3], recv_sem=swap_recv.at[3],
        device_id={"ka": other}, device_id_type=MESH,
    )
    give.start()
    finish(core)
    keep = pltpu.make_async_copy(obuf.at[my_rows], out_ref.at[:, my_columns], local_sem.at[3])
    keep.start()

    def drain(way, far, near, a, m):
        message(way, far * n_y + near, a, m).wait_send()

    def drain_line(way):
        def body(far, carry):
            for a in range(n_ka):
                for m in early:
                    drain(way, far, y, a, m)
                for near in range(n_y):
                    drain(way, far, near, a, last)
            return carry
        return body

    lax.fori_loop(jnp.where(has_left, z, n_z), n_z, drain_line(LEFT), 0)
    lax.fori_loop(0, jnp.where(has_right, z + 1, 0), drain_line(RIGHT), 0)

    def drain_across(far, carry):
        for a in range(n_ka):
            for m in early:
                drain(ACROSS, far, y, a, m)
        return carry

    lax.fori_loop(0, n_z, drain_across, 0)
    for a in range(n_ka):
        drain(ACROSS, z, y, a, last)
    for item in swaps_out:
        item.wait_send()
    give.wait_send()
    keep.wait()
    pltpu.make_async_remote_copy(
        src_ref=obuf.at[other_rows], dst_ref=out_ref.at[:, other_columns],
        send_sem=swap_send.at[3], recv_sem=swap_recv.at[3],
        device_id={"ka": other}, device_id_type=MESH,
    ).wait_recv()


def solution(mesh):
    n_pb, n_ka = mesh.shape["pb"], mesh.shape["ka"]
    width = 2

    def local(queries, keys, values, block_pairs):
        rows = queries.shape[0]
        tile = n_ka * rows
        shards = block_pairs.shape[2]
        anywhere = pl.BlockSpec(memory_space=pl.ANY)
        return pl.pallas_call(
            functools.partial(kernel, n_pb, n_ka, width),
            out_shape=jax.ShapeDtypeStruct(queries.shape, queries.dtype),
            in_specs=[anywhere, anywhere, anywhere, pl.BlockSpec(memory_space=pltpu.VMEM)],
            out_specs=anywhere,
            scratch_shapes=[
                pltpu.VMEM((tile, HEAD), jnp.bfloat16),
                pltpu.VMEM((n_pb, tile, HEAD), jnp.bfloat16),
                pltpu.VMEM((n_pb, tile, HEAD), jnp.bfloat16),
                pltpu.VMEM((rows // BLOCK, shards, tile), jnp.float32),
                pltpu.VMEM((1, tile), jnp.float32),
                pltpu.VMEM((1, tile), jnp.float32),
                pltpu.VMEM((HEAD, tile), jnp.float32),
                pltpu.VMEM((tile, HEAD), jnp.bfloat16),
                pltpu.VMEM((HEAD, tile), jnp.bfloat16),
                pltpu.SemaphoreType.DMA((3, n_pb, n_ka, 4)),
                pltpu.SemaphoreType.DMA((n_pb, n_ka, 4)),
                pltpu.SemaphoreType.DMA((4,)),
                pltpu.SemaphoreType.DMA((4,)),
                pltpu.SemaphoreType.DMA((4,)),
            ],
            compiler_params=pltpu.CompilerParams(collective_id=0, has_side_effects=True),
        )(queries, keys, values, block_pairs.transpose(0, 3, 1, 2))

    rows_spec = P(("groups", "pb", "ka"), None)
    return jax.shard_map(
        local, mesh=mesh,
        in_specs=(rows_spec, rows_spec, rows_spec, P("groups", "pb", None, None)),
        out_specs=rows_spec, check_vma=False,
    )
```

```python
import functools
import math

import jax
import jax.numpy as jnp
from jax import lax
from jax.experimental import pallas as pl
from jax.experimental.pallas import tpu as pltpu
from jax.sharding import PartitionSpec as P

HEAD = 128
HEADS = 2
BLOCK = 128
NEGATIVE_FILL = -1e30
EXP2_SCALE = HEAD ** (-0.5) * math.log2(math.e)
MESH = pl.DeviceIdType.MESH
LEFT, RIGHT, ACROSS = 0, 1, 2


def kernel(
    n_pb, n_ka, width, q_ref, k_ref, v_ref, pairs_ref, out_ref,
    qbuf, kbuf, vbuf, bias, peak, total, accum, obuf, qturned,
    send_sem, recv_sem, local_sem, swap_send, swap_recv,
):
    rows = q_ref.shape[0]
    tile = n_ka * rows
    late = BLOCK - BLOCK // 4
    half = (rows - late) // 2
    n_y = width
    n_z = n_pb // n_y
    core = lax.axis_index("ka")
    place = lax.axis_index("pb")
    z, y = place // n_y, place % n_y
    other = 1 - core
    across = z * n_y + (1 - y)
    has_left, has_right = z > 0, z < n_z - 1
    targets = {LEFT: place - n_y, RIGHT: place + n_y, ACROSS: across}

    barrier = pltpu.get_barrier_semaphore()
    pl.semaphore_signal(barrier, inc=1, device_id={"ka": other}, device_id_type=MESH)
    pl.semaphore_signal(barrier, inc=1, device_id={"pb": across}, device_id_type=MESH)

    @pl.when(has_left)
    def _():
        pl.semaphore_signal(barrier, inc=1, device_id={"pb": place - n_y}, device_id_type=MESH)

    @pl.when(has_right)
    def _():
        pl.semaphore_signal(barrier, inc=1, device_id={"pb": place + n_y}, device_id_type=MESH)

    my_columns = pl.ds(pl.multiple_of(core * HEAD, HEAD), HEAD)
    other_columns = pl.ds(pl.multiple_of(other * HEAD, HEAD), HEAD)
    my_rows = pl.ds(pl.multiple_of(core * rows, BLOCK), rows)
    other_rows = pl.ds(pl.multiple_of(other * rows, BLOCK), rows)

    stage = [
        pltpu.make_async_copy(k_ref.at[:, my_columns], kbuf.at[place, my_rows], local_sem.at[0]),
        pltpu.make_async_copy(v_ref.at[:, my_columns], vbuf.at[place, my_rows], local_sem.at[1]),
        pltpu.make_async_copy(q_ref.at[:, my_columns], qbuf.at[my_rows], local_sem.at[2]),
    ]
    for item in stage:
        item.start()

    pl.semaphore_wait(
        barrier, 2 + has_left.astype(jnp.int32) + has_right.astype(jnp.int32)
    )

    def swap(index, source, target):
        return pltpu.make_async_remote_copy(
            src_ref=source, dst_ref=target, send_sem=swap_send.at[index],
            recv_sem=swap_recv.at[index], device_id={"ka": other}, device_id_type=MESH,
        )

    swaps_out = [
        swap(0, k_ref.at[:, other_columns], kbuf.at[place, my_rows]),
        swap(1, v_ref.at[:, other_columns], vbuf.at[place, my_rows]),
        swap(2, q_ref.at[:, other_columns], qbuf.at[my_rows]),
    ]
    for item in swaps_out:
        item.start()

    spans = ((0, rows), (0, half), (half, half), (2 * half, late))
    early, last = (0, 1, 2), 3

    def part(p, a, m):
        start, size = spans[m]
        span = pl.ds(pl.multiple_of(a * rows + start, 16), size)
        return (vbuf if m else kbuf).at[p, span]

    def message(way, p, a, m, source=None):
        ref = part(p, a, m)
        return pltpu.make_async_remote_copy(
            src_ref=ref if source is None else source, dst_ref=ref, send_sem=send_sem.at[way, p, a, m],
            recv_sem=recv_sem.at[p, a, m], device_id={"pb": targets[way]}, device_id_type=MESH,
        )

    def send(way, p, a, m, source=None):
        if way == ACROSS:
            message(way, p, a, m, source).start()
        else:
            @pl.when(has_left if way == LEFT else has_right)
            def _():
                message(way, p, a, m, source).start()

    def arrive(p, a, m):
        message(ACROSS, p, a, m).wait_recv()

    def send_own(a, parts, source=None, ways=(ACROSS, LEFT, RIGHT)):
        for m in parts:
            start, size = spans[m]
            view = None if source is None else source.at[pl.ds(start, size), my_columns]
            for way in ways:
                send(way, place, a, m, view)

    send_own(core, (0,), k_ref)
    send_own(core, (last,), v_ref, (ACROSS,))
    send_own(core, (1, 2), v_ref)

    swap(0, k_ref.at[:, other_columns], kbuf.at[place, other_rows]).wait_recv()
    send_own(other, (0,))
    swap(1, v_ref.at[:, other_columns], vbuf.at[place, other_rows]).wait_recv()
    send_own(other, (last,), None, (ACROSS,))
    send_own(other, (1, 2))
    send_own(core, (last,), v_ref, (LEFT, RIGHT))
    send_own(other, (last,), None, (LEFT, RIGHT))
    codes = pairs_ref[core, :, 0, :].T
    shards = codes.shape[0]
    query_block = lax.broadcasted_iota(jnp.int32, (shards, tile), 1) // BLOCK
    blocks = rows // BLOCK
    kept = [None] * blocks
    for slot in range(codes.shape[1]):
        column = jnp.broadcast_to(codes[:, slot : slot + 1], (shards, tile))
        for j in range(blocks):
            hit = column == query_block * blocks + j
            kept[j] = hit if kept[j] is None else kept[j] | hit
    for j in range(blocks):
        bias[j] = jnp.where(kept[j], 0.0, NEGATIVE_FILL).astype(jnp.float32)
    peak[...] = jnp.full_like(peak, NEGATIVE_FILL)
    total[...] = jnp.zeros_like(total)
    accum[...] = jnp.zeros_like(accum)

    for item in stage:
        item.wait()
    swap(2, q_ref.at[:, other_columns], qbuf.at[other_rows]).wait_recv()

    qturned[...] = qbuf[...].T
    lanes = tile

    def attend(p, first=0, count=n_ka):
        keys = pl.ds(first * rows, count * rows)
        turned = vbuf[p, keys].T
        for start in range(0, tile, lanes):
            span = pl.ds(start, lanes)
            scores = lax.dot_general(
                kbuf[p, keys], qturned[:, span], (((1,), (0,)), ((), ())),
                preferred_element_type=jnp.float32,
            )
            masked = []
            for a in range(count):
                for j in range(blocks):
                    row = (a * blocks + j) * BLOCK
                    line = bias[j, pl.ds(p * n_ka + first + a, 1), span]
                    masked.append(scores[row : row + BLOCK] + line)
            scores = jnp.concatenate(masked, axis=0)
            before = peak[:, span]
            after = jnp.maximum(before, scores.max(0, keepdims=True))
            rescale = jnp.exp2((before - after) * EXP2_SCALE)
            chances = jnp.exp2((scores - after) * EXP2_SCALE)
            peak[:, span] = after
            total[:, span] = total[:, span] * rescale + chances.sum(0, keepdims=True)
            accum[:, span] = accum[:, span] * rescale + lax.dot_general(
                turned, chances.astype(jnp.bfloat16), (((1,), (0,)), ((), ())),
                preferred_element_type=jnp.float32,
            )

    attend(place)

    for a in range(n_ka):
        arrive(across, a, last)
        send(LEFT, across, a, last)
        send(RIGHT, across, a, last)

    def sides(step):
        return ((z - step, z - step >= 0, RIGHT), (z + step, z + step < n_z, LEFT))

    def attend_across(p):
        for a in range(n_ka):
            for m in early:
                arrive(p, a, m)
        attend(p)

    def forward_early(step):
        for a in range(n_ka):
            for m in early:
                for far, valid, way in sides(step):
                    @pl.when(valid)
                    def _(far=far, way=way):
                        p = far * n_y + y
                        arrive(p, a, m)
                        send(way, p, a, m)
                        send(ACROSS, p, a, m)

    def forward_last(step):
        for a in range(n_ka):
            for far, valid, way in sides(step):
                @pl.when(valid)
                def _(far=far, way=way):
                    for near in (y, 1 - y):
                        p = far * n_y + near
                        arrive(p, a, last)
                        send(way, p, a, last)

    def across_sides(step):
        for far, valid, _ in sides(step):
            @pl.when(valid)
            def _(far=far):
                attend_across(far * n_y + 1 - y)

    def near_sides(step):
        for far, valid, _ in sides(step):
            @pl.when(valid)
            def _(far=far):
                attend(far * n_y + y)

    at_end = jnp.logical_not(jnp.logical_and(has_left, has_right))
    forward_early(1)
    forward_last(1)
    attend_across(across)

    def one_step(step, carry):
        @pl.when(at_end)
        def _():
            near_sides(step)

        @pl.when(step < n_z - 1)
        def _():
            forward_early(step + 1)

        @pl.when(at_end)
        def _():
            across_sides(step)

        @pl.when(step < n_z - 1)
        def _():
            forward_last(step + 1)

        @pl.when(jnp.logical_not(at_end))
        def _():
            near_sides(step)
            across_sides(step)
        return carry

    lax.fori_loop(1, n_z, one_step, 0)

    def finish(which):
        span = pl.ds(pl.multiple_of(which * rows, BLOCK), rows)
        done = accum[:, span] / total[:, span]
        obuf[span, :] = done.T.astype(obuf.dtype)

    finish(other)
    give = pltpu.make_async_remote_copy(
        src_ref=obuf.at[other_rows], dst_ref=out_ref.at[:, my_columns],
        send_sem=swap_send.at[3], recv_sem=swap_recv.at[3],
        device_id={"ka": other}, device_id_type=MESH,
    )
    give.start()
    finish(core)
    keep = pltpu.make_async_copy(obuf.at[my_rows], out_ref.at[:, my_columns], local_sem.at[3])
    keep.start()

    def drain(way, far, near, a, m):
        message(way, far * n_y + near, a, m).wait_send()

    def drain_line(way):
        def body(far, carry):
            for a in range(n_ka):
                for m in early:
                    drain(way, far, y, a, m)
                for near in range(n_y):
                    drain(way, far, near, a, last)
            return carry
        return body

    lax.fori_loop(jnp.where(has_left, z, n_z), n_z, drain_line(LEFT), 0)
    lax.fori_loop(0, jnp.where(has_right, z + 1, 0), drain_line(RIGHT), 0)

    def drain_across(far, carry):
        for a in range(n_ka):
            for m in early:
                drain(ACROSS, far, y, a, m)
        return carry

    lax.fori_loop(0, n_z, drain_across, 0)
    for a in range(n_ka):
        drain(ACROSS, z, y, a, last)
    for item in swaps_out:
        item.wait_send()
    give.wait_send()
    keep.wait()
    pltpu.make_async_remote_copy(
        src_ref=obuf.at[other_rows], dst_ref=out_ref.at[:, other_columns],
        send_sem=swap_send.at[3], recv_sem=swap_recv.at[3],
        device_id={"ka": other}, device_id_type=MESH,
    ).wait_recv()


def solution(mesh):
    n_pb, n_ka = mesh.shape["pb"], mesh.shape["ka"]
    width = 2

    def local(queries, keys, values, block_pairs):
        rows = queries.shape[0]
        tile = n_ka * rows
        shards = block_pairs.shape[2]
        anywhere = pl.BlockSpec(memory_space=pl.ANY)
        return pl.pallas_call(
            functools.partial(kernel, n_pb, n_ka, width),
            out_shape=jax.ShapeDtypeStruct(queries.shape, queries.dtype),
            in_specs=[anywhere, anywhere, anywhere, pl.BlockSpec(memory_space=pltpu.VMEM)],
            out_specs=anywhere,
            scratch_shapes=[
                pltpu.VMEM((tile, HEAD), jnp.bfloat16),
                pltpu.VMEM((n_pb, tile, HEAD), jnp.bfloat16),
                pltpu.VMEM((n_pb, tile, HEAD), jnp.bfloat16),
                pltpu.VMEM((rows // BLOCK, shards, tile), jnp.float32),
                pltpu.VMEM((1, tile), jnp.float32),
                pltpu.VMEM((1, tile), jnp.float32),
                pltpu.VMEM((HEAD, tile), jnp.float32),
                pltpu.VMEM((tile, HEAD), jnp.bfloat16),
                pltpu.VMEM((HEAD, tile), jnp.bfloat16),
                pltpu.SemaphoreType.DMA((3, n_pb, n_ka, 4)),
                pltpu.SemaphoreType.DMA((n_pb, n_ka, 4)),
                pltpu.SemaphoreType.DMA((4,)),
                pltpu.SemaphoreType.DMA((4,)),
                pltpu.SemaphoreType.DMA((4,)),
            ],
            compiler_params=pltpu.CompilerParams(collective_id=0, has_side_effects=True),
        )(queries, keys, values, block_pairs.transpose(0, 3, 1, 2))

    rows_spec = P(("groups", "pb", "ka"), None)
    return jax.shard_map(
        local, mesh=mesh,
        in_specs=(rows_spec, rows_spec, rows_spec, P("groups", "pb", None, None)),
        out_specs=rows_spec, check_vma=False,
    )
```
